32 devices in a mesh: gx: 4 (over x, core), gy: 8 (over z, y).
Axes of the slice: x: 2, y: 2, z: 4, core: 2. Of those that a mesh axis runs over, the one named last changes fastest.
Arguments:
- activation: bfloat16 [32, 16, 32, 128], P(None, 'gx', 'gy'), may hold values from -6 to 6
- out_grad: bfloat16 [32, 16, 32, 128], P(None, 'gx', 'gy'), may hold values from -6 to 6
- kernel: bfloat16 [3, 3, 3, 32, 32], replicated, may hold values from -0.21875 to 0.21875
Outputs:
- grad_input: bfloat16 [32, 16, 32, 128], P(None, 'gx', 'gy')
- grad_kernel: float32 [3, 3, 3, 32, 32], replicated
The draws below stay inside these ranges and needn't reach their ends.
All inputs are finite; a program needn't handle non-finite values.
Results may differ from the reference program's by a relative error of at most 0.001.
Values may be sent and summed in bfloat16 or wider, within the bound.
No kernel may reach another device: no remote copies, remote signals or barrier semaphores. Data moves between devices by JAX's collectives and lax.ppermute only.
A program may use at most 64 MiB of HBM per device.

```python
import jax
import jax.numpy as jnp

C = 32
NZ = 128
NX = 16
NY = 32


def shard_levels(stream_key, dims, shards, low, high):
    level = 1.0
    for dim, parts in shards:
        steps = jax.random.uniform(jax.random.fold_in(jax.random.fold_in(stream_key, 6), dim), (parts,), jnp.float32, low / len(shards), high / len(shards))
        level = level * jnp.repeat(jnp.exp(steps), dims[dim] // parts).reshape((-1,) + (1,) * (len(dims) - 1 - dim))
    return level


def bell_draw(stream_key, dims, spread, reach, shards=(), held_as=jnp.bfloat16):
    level = shard_levels(stream_key, dims, shards, -0.22, 0.18) if shards else 1.0
    values = jax.random.normal(stream_key, dims, jnp.float32) * spread * level
    return jnp.minimum(jnp.maximum(values, -reach), reach).astype(held_as)


def setup_inputs(seed: int = 0) -> dict:
    key_list = jax.random.split(jax.random.key(seed), 4)
    return {
        "activation": bell_draw(key_list[0], (C, NX, NY, NZ), 1.0, 6.0, ((1, 4), (2, 8))),
        "out_grad": bell_draw(key_list[1], (C, NX, NY, NZ), 1.0, 6.0, ((1, 4), (2, 8))),
        "kernel": bell_draw(key_list[2], (3, 3, 3, C, C), (27 * C) ** -0.5, 0.21875),
    }


def reference(activation, out_grad, kernel):
    channels = activation.shape[0]
    size_x, size_y, size_z = (activation.shape[1], activation.shape[2], activation.shape[3])
    cell_count = size_x * size_y * size_z
    grad_pad = jnp.pad(out_grad, ((0, 0), (1, 1), (1, 1), (1, 1)))
    act_pad = jnp.pad(activation, ((0, 0), (1, 1), (1, 1), (1, 1)))
    flat_grad = out_grad.reshape(channels, cell_count)
    accumulated = jnp.zeros((channels, cell_count), jnp.float32)
    products = []
    for off_x in range(3):
        for off_y in range(3):
            for off_z in range(3):
                window = grad_pad[:, 2 - off_x:2 - off_x + size_x, 2 - off_y:2 - off_y + size_y, 2 - off_z:2 - off_z + size_z].reshape(channels, cell_count)
                accumulated = accumulated + jnp.dot(kernel[off_x, off_y, off_z].T, window, preferred_element_type=jnp.float32)
                shifted = act_pad[:, off_x:off_x + size_x, off_y:off_y + size_y, off_z:off_z + size_z].reshape(channels, cell_count)
                products.append(jnp.dot(flat_grad, shifted.T, preferred_element_type=jnp.float32))
    grad_input = accumulated.reshape(channels, size_x, size_y, size_z).astype(jnp.bfloat16)
    raw = jnp.stack(products).reshape(3, 3, 3, channels, channels)
    grad_kernel = raw / jnp.sqrt(jnp.float32(NX * NY * NZ))
    return (grad_input, grad_kernel)
```

```python
import functools

import jax
import jax.numpy as jnp
from jax import lax
from jax.experimental import pallas as pl
from jax.experimental.pallas import tpu as pltpu
from jax.sharding import PartitionSpec as P

BOTH = ("gx", "gy")
VMEM = pl.BlockSpec(memory_space=pltpu.VMEM)
BF16, F32 = jnp.bfloat16, jnp.float32


def params():
    return pltpu.CompilerParams(vmem_limit_bytes=16 << 20)


def cost(flops, nbytes):
    return pl.CostEstimate(flops=flops, bytes_accessed=nbytes, transcendentals=0)


def pairs(counts, partner):
    nx, ny = counts
    flat = []
    for ix in range(nx):
        for iy in range(ny):
            jx, jy = partner(ix, iy)
            flat.append((ix * ny + iy, jx * ny + jy))
    return flat


def shift_z(cells, step):
    size = cells.shape[-1]
    lane = lax.broadcasted_iota(jnp.int32, cells.shape, cells.ndim - 1)
    moved = pltpu.roll(cells, step % size, cells.ndim - 1)
    return jnp.where(lane == (0 if step == 1 else size - 1), 0.0, moved)


def prepare_body(act_ref, grad_ref, act_out, grad_out, near_out, far_out):
    channels, size_x, size_y, size_z = grad_ref.shape
    right = lax.axis_index("gx") % 2 == 0
    for x in range(size_x):
        grad = jnp.swapaxes(grad_ref[:, x].astype(F32), 0, 1).astype(BF16)
        grad_out[x] = grad
    near_out[...] = grad_out[jnp.where(right, size_x - 1, 0)]
    far_out[...] = grad_out[jnp.where(right, 0, size_x - 1)]
    for x in range(size_x):
        act = jnp.swapaxes(act_ref[:, x].astype(F32), 0, 1)
        act_out[x, :, :channels] = shift_z(act, 1).astype(BF16)
        act_out[x, :, channels : 2 * channels] = act.astype(BF16)
        act_out[x, :, 2 * channels :] = shift_z(act, -1).astype(BF16)


def faces_body(grad_ref, near_ref, far_ref, left_out, right_out, near_out, far_out):
    size_x, size_y = grad_ref.shape[:2]
    ix, iy = lax.axis_index("gx"), lax.axis_index("gy")
    even = ix % 2 == 0
    zero = jnp.zeros(near_ref.shape, BF16)
    near, far = near_ref[...], far_ref[...]
    left = jnp.where(even, far, near)
    right = jnp.where(even, near, far)
    left_out[...] = jnp.where(ix == 0, zero, left)
    right_out[...] = jnp.where(ix == lax.axis_size("gx") - 1, zero, right)
    high = jnp.where(iy % 2 == 0, size_y - 1, 0)
    low = size_y - 1 - high
    for out, y in ((near_out, high), (far_out, low)):
        out[0] = left_out[y]
        out[size_x + 1] = right_out[y]
        for x in range(size_x):
            out[x + 1] = grad_ref[x, y]


def columns(grad_ref, left_ref, right_ref, near_ref, far_ref):
    size_x, size_y = grad_ref.shape[:2]
    iy = lax.axis_index("gy")
    even = iy % 2 == 0

    def column(x, y):
        if y < 0:
            face = jnp.where(even, far_ref[x + 1], near_ref[x + 1])
            return jnp.where(iy == 0, jnp.zeros_like(face), face)
        if y >= size_y:
            face = jnp.where(even, near_ref[x + 1], far_ref[x + 1])
            return jnp.where(iy == lax.axis_size("gy") - 1, jnp.zeros_like(face), face)
        if x < 0:
            return left_ref[y]
        if x >= size_x:
            return right_ref[y]
        return grad_ref[x, y]

    return column


def fill_halo(grad_ref, left_ref, right_ref, near_ref, far_ref, cells):
    size_x, size_y = grad_ref.shape[:2]
    column = columns(grad_ref, left_ref, right_ref, near_ref, far_ref)
    for x in range(-1, size_x + 1):
        for y in range(-1, size_y + 1):
            cells[x + 1, y + 1] = column(x, y)


def stacked(cells, x, y):
    return jnp.concatenate([cells[x - a + 2, y - b + 2] for a in range(3) for b in range(3)], axis=0)


def half_of():
    bits = lax.axis_index("gx") ^ (lax.axis_index("gy"))
    width = max(lax.axis_size("gx"), lax.axis_size("gy")).bit_length()
    parity = bits & 1
    for k in range(1, width):
        parity = parity ^ ((bits >> k) & 1)
    return parity


def weights_body(act_ref, grad_ref, left_ref, right_ref, near_ref, far_ref, send_out, keep_out, cells, total):
    size_x, size_y, rows3, size_z = act_ref.shape
    channels = rows3 // 3
    fill_halo(grad_ref, left_ref, right_ref, near_ref, far_ref, cells)
    acc = jnp.zeros((9 * channels, rows3), F32)
    for x in range(size_x):
        for y in range(0, size_y, 2):
            lhs = jnp.concatenate([stacked(cells, x, y), stacked(cells, x, y + 1)], axis=1)
            rhs = jnp.concatenate([act_ref[x, y], act_ref[x, y + 1]], axis=1)
            acc = acc + lax.dot_general(lhs, rhs, (((1,), (1,)), ((), ())), preferred_element_type=F32)
    rows = 9 * channels // 4
    spread = [acc[3 * rows :, k * channels : (k + 1) * channels] for k in range(3)]
    dense = jnp.concatenate([acc[: 3 * rows], jnp.concatenate(spread, axis=0)], axis=1)
    total[: 3 * rows] = dense
    half = total.shape[0] // 2
    total[3 * rows :] = jnp.zeros((total.shape[0] - 3 * rows, total.shape[1]), F32)
    mine = half_of()
    keep_out[...] = total[pl.ds(pl.multiple_of(mine * half, 8), half)]
    send_out[...] = total[pl.ds(pl.multiple_of((1 - mine) * half, 8), half)]


def finish_body(scale, mine_ref, other_ref, out_ref, total):
    channels = out_ref.shape[-1]
    half = mine_ref.shape[0]
    mine = half_of()
    total[pl.ds(pl.multiple_of(mine * half, 8), half)] = mine_ref[...] / scale
    total[pl.ds(pl.multiple_of((1 - mine) * half, 8), half)] = other_ref[...] / scale
    rows = 9 * channels // 4
    for ab in range(9):
        for c in range(3):
            first = ab * channels
            parts = []
            for r in range(first, first + channels, 8):
                if r < 3 * rows:
                    parts.append(total[r : r + 8, c * channels : (c + 1) * channels])
                else:
                    q = c * rows + r - 3 * rows
                    parts.append(total[q : q + 8, 3 * channels : 4 * channels])
            out_ref[ab // 3, ab % 3, c] = jnp.concatenate(parts, axis=0)


def inputs_body(grad_ref, left_ref, right_ref, near_ref, far_ref, kernel_ref, out_ref, cells):
    channels, size_x, size_y, size_z = out_ref.shape
    fill_halo(grad_ref, left_ref, right_ref, near_ref, far_ref, cells)
    taps = jnp.concatenate(
        [
            jnp.concatenate([kernel_ref[a, b, c] for a in range(3) for b in range(3)], axis=0).astype(F32)
            for c in range(3)
        ],
        axis=1,
    )
    taps = jnp.transpose(taps).astype(BF16)
    for x in range(size_x):
        rows = []
        for y in range(0, size_y, 2):
            rhs = jnp.concatenate([stacked(cells, x, y), stacked(cells, x, y + 1)], axis=1)
            terms = jnp.dot(taps, rhs, preferred_element_type=F32)
            for k in range(2):
                part = terms[:, k * size_z : (k + 1) * size_z]
                row = shift_z(part[:channels], -1) + part[channels : 2 * channels]
                rows.append(row + shift_z(part[2 * channels :], 1))
        out_ref[:, x] = jnp.swapaxes(jnp.stack(rows), 0, 1).astype(BF16)


def shards(activation, out_grad, kernel):
    channels, size_x, size_y, size_z = activation.shape
    counts = (lax.axis_size("gx"), lax.axis_size("gy"))
    nx, ny = counts
    shape = jax.ShapeDtypeStruct
    volume = channels * size_x * size_y * size_z

    def permute(value, partner):
        return lax.ppermute(value, BOTH, pairs(counts, partner))

    def odd_y(ix, iy):
        if iy in (0, ny - 1):
            return ix ^ 1, iy
        return ix, (iy + 1 if iy % 2 else iy - 1)

    def odd_x(ix, iy):
        return (ix + 1 if ix % 2 else ix - 1) % nx, iy

    face = shape((size_y, channels, size_z), BF16)
    long_face = shape((size_x + 2, channels, size_z), BF16)
    act, grad, near, far = pl.pallas_call(
        prepare_body,
        out_shape=(
            shape((size_x, size_y, 3 * channels, size_z), BF16),
            shape((size_x, size_y, channels, size_z), BF16),
            face,
            face,
        ),
        in_specs=[VMEM] * 2,
        out_specs=(VMEM,) * 4,
        compiler_params=params(),
        cost_estimate=cost(0, 12 * volume),
        name="prepare",
    )(activation, out_grad)
    far = permute(far, odd_x)
    near = permute(near, lambda ix, iy: (ix ^ 1, iy))
    left, right, near, far = pl.pallas_call(
        faces_body,
        out_shape=(face, face, long_face, long_face),
        in_specs=[VMEM] * 3,
        out_specs=(VMEM,) * 4,
        compiler_params=params(),
        cost_estimate=cost(0, 4 * volume),
        name="faces",
    )(grad, near, far)
    far = permute(far, odd_y)
    near = permute(near, lambda ix, iy: (ix, iy ^ 1))
    halo = [pltpu.VMEM((size_x + 2, size_y + 2, channels, size_z), BF16)]
    rows = (9 * 3 * channels * channels // 128 + 15) // 16 * 8
    half = shape((rows, 128), F32)
    send, total = pl.pallas_call(
        weights_body,
        out_shape=(half, half),
        in_specs=[VMEM] * 6,
        out_specs=(VMEM,) * 2,
        scratch_shapes=halo + [pltpu.VMEM((2 * rows, 128), F32)],
        compiler_params=params(),
        cost_estimate=cost(54 * channels * volume, 12 * volume),
        name="weights",
    )(act, grad, left, right, near, far)
    total = total + permute(send, lambda ix, iy: (ix ^ 1, iy))
    step = 2
    while step < nx:
        total = total + permute(total, lambda ix, iy: (ix ^ 1 ^ step, iy))
        step *= 2
    step = 1
    while step < ny:
        total = total + permute(total, lambda ix, iy: (ix ^ 1, iy ^ step))
        step *= 2
    grad_input = pl.pallas_call(
        inputs_body,
        out_shape=shape(activation.shape, BF16),
        in_specs=[VMEM] * 6,
        out_specs=VMEM,
        scratch_shapes=halo,
        compiler_params=params(),
        cost_estimate=cost(54 * channels * volume, 12 * volume),
        name="inputs",
    )(grad, left, right, near, far, kernel)
    other = permute(total, lambda ix, iy: (ix ^ 1, iy))
    cell_count = nx * size_x * ny * size_y * size_z
    grad_kernel = pl.pallas_call(
        functools.partial(finish_body, float(cell_count) ** 0.5),
        out_shape=shape(kernel.shape, F32),
        in_specs=[VMEM] * 2,
        out_specs=VMEM,
        scratch_shapes=[pltpu.VMEM((2 * rows, 128), F32)],
        compiler_params=params(),
        name="finish",
    )(total, other)
    return (grad_input, grad_kernel)


def solution(mesh):
    return jax.shard_map(
        shards,
        mesh=mesh,
        in_specs=(P(None, "gx", "gy", None), P(None, "gx", "gy", None), P()),
        out_specs=(P(None, "gx", "gy", None), P()),
        check_vma=False,
    )
```

```python
import functools

import jax
import jax.numpy as jnp
from jax import lax
from jax.experimental import pallas as pl
from jax.experimental.pallas import tpu as pltpu
from jax.sharding import PartitionSpec as P

BOTH = ("gx", "gy")
VMEM = pl.BlockSpec(memory_space=pltpu.VMEM)
BF16, F32 = jnp.bfloat16, jnp.float32


def params(limit=16 << 20):
    return pltpu.CompilerParams(vmem_limit_bytes=limit)


def cost(flops, nbytes):
    return pl.CostEstimate(flops=flops, bytes_accessed=nbytes, transcendentals=0)


def pairs(counts, partner):
    nx, ny = counts
    flat = []
    for ix in range(nx):
        for iy in range(ny):
            jx, jy = partner(ix, iy)
            flat.append((ix * ny + iy, jx * ny + jy))
    return flat


def shift_z(cells, step):
    size = cells.shape[-1]
    lane = lax.broadcasted_iota(jnp.int32, cells.shape, cells.ndim - 1)
    moved = pltpu.roll(cells, step % size, cells.ndim - 1)
    return jnp.where(lane == (0 if step == 1 else size - 1), 0.0, moved)


def gradient_body(grad_hbm, grad_out, near_out, held, sems):
    size_x = grad_out.shape[0]
    copies = [pltpu.make_async_copy(grad_hbm.at[:, x], held.at[x], sems.at[x]) for x in range(size_x)]
    for copy in copies:
        copy.start()
    for x, copy in enumerate(copies):
        copy.wait()
        grad_out[x] = jnp.swapaxes(held[x].astype(F32), 0, 1).astype(BF16)
    near_out[...] = grad_out[jnp.where(lax.axis_index("gx") % 2 == 0, size_x - 1, 0)]


def activation_body(act_ref, act_out):
    channels, size_x = act_ref.shape[:2]
    for x in range(size_x):
        act = jnp.swapaxes(act_ref[:, x].astype(F32), 0, 1)
        act_out[x, :, :channels] = shift_z(act, 1).astype(BF16)
        act_out[x, :, channels : 2 * channels] = act.astype(BF16)
        act_out[x, :, 2 * channels :] = shift_z(act, -1).astype(BF16)


def faces_body(grad_ref, near_ref, even_out, odd_out):
    size_x, size_y = grad_ref.shape[:2]
    high = jnp.where(lax.axis_index("gy") % 2 == 0, size_y - 1, 0)
    for out, y in ((even_out, high), (odd_out, size_y - 1 - high)):
        for x in range(size_x):
            out[x] = grad_ref[x, y]
        out[size_x] = near_ref[y]


def half_of():
    bits = lax.axis_index("gx") ^ lax.axis_index("gy")
    width = max(lax.axis_size("gx"), lax.axis_size("gy")).bit_length()
    parity = bits & 1
    for k in range(1, width):
        parity = parity ^ ((bits >> k) & 1)
    return parity


def stacked(cells, x, y):
    return jnp.concatenate([cells[x - a + 2, y - b + 2] for a in range(3) for b in range(3)], axis=0)


def pack(terms, total):
    channels = terms.shape[1] // 3
    rows = 9 * channels // 4
    spread = [terms[3 * rows :, k * channels : (k + 1) * channels] for k in range(3)]
    total[: 3 * rows] = jnp.concatenate([terms[: 3 * rows], jnp.concatenate(spread, axis=0)], axis=1)
    total[3 * rows :] = jnp.zeros((total.shape[0] - 3 * rows, total.shape[1]), F32)


def split(total, send_out, keep_out):
    half = keep_out.shape[0]
    mine = half_of()
    keep_out[...] = total[pl.ds(pl.multiple_of(mine * half, 8), half)]
    send_out[...] = total[pl.ds(pl.multiple_of((1 - mine) * half, 8), half)]


def weights_body(act_ref, grad_ref, near_ref, even_ref, odd_ref, cells, far_out, send_out, keep_out, total):
    size_x, size_y, rows3, size_z = act_ref.shape
    channels = rows3 // 3
    ix, iy = lax.axis_index("gx"), lax.axis_index("gy")
    near = jnp.where(ix % 2 == 0, size_x + 1, 0)
    zero = jnp.zeros((channels, size_z), BF16)
    for x in range(size_x + 1):
        at = x + 1 if x < size_x else near
        for y in range(size_y):
            cells[at, y + 1] = grad_ref[x, y] if x < size_x else near_ref[y]
        low = jnp.where(iy % 2 == 0, odd_ref[x], even_ref[x])
        high = jnp.where(iy % 2 == 0, even_ref[x], odd_ref[x])
        cells[at, 0] = jnp.where(iy == 0, zero, low)
        cells[at, size_y + 1] = jnp.where(iy == lax.axis_size("gy") - 1, zero, high)
    for y in range(size_y + 2):
        cells[size_x + 1 - near, y] = zero
    edge = jnp.where(ix % 2 == 0, 0, size_x - 1)
    far_out[: size_y + 2] = cells[edge + 1]
    for y in range(size_y):
        far_out[size_y + 2 + y] = act_ref[edge, y, channels : 2 * channels]
    acc = jnp.zeros((9 * channels, rows3), F32)
    for x in range(size_x):
        for y in range(0, size_y, 2):
            lhs = jnp.concatenate([stacked(cells, x, y), stacked(cells, x, y + 1)], axis=1)
            rhs = jnp.concatenate([act_ref[x, y], act_ref[x, y + 1]], axis=1)
            acc = acc + lax.dot_general(lhs, rhs, (((1,), (1,)), ((), ())), preferred_element_type=F32)
    pack(acc, total)
    split(total, send_out, keep_out)


def across_body(both, act_ref, cells, far_ref, send_out, keep_out, total):
    size_x, size_y, rows3, size_z = act_ref.shape
    channels = rows3 // 3
    ix = lax.axis_index("gx")
    even = ix % 2 == 0
    edge = jnp.where(even, 0, size_x - 1)

    def product(grads, acts):
        acc = jnp.zeros((3 * channels, rows3), F32)
        for y in range(0, size_y, 2):
            lhs = [jnp.concatenate([grads(y + k - b + 2) for b in range(3)], axis=0) for k in range(2)]
            rhs = [acts(y), acts(y + 1)]
            acc = acc + lax.dot_general(
                jnp.concatenate(lhs, axis=1),
                jnp.concatenate(rhs, axis=1),
                (((1,), (1,)), ((), ())),
                preferred_element_type=F32,
            )
        return acc

    def offsets(y):
        act = far_ref[size_y + 2 + y].astype(F32)
        return jnp.concatenate([shift_z(act, 1), act, shift_z(act, -1)], axis=0).astype(BF16)

    own = product(lambda y: far_ref[y], lambda y: act_ref[edge, y])
    other = product(lambda y: cells[edge + 1, y], offsets) if both else jnp.zeros_like(own)
    outside = (ix == 0) | (ix == lax.axis_size("gx") - 1)
    first = jnp.where(outside, 0.0, jnp.where(even, other, own))
    last = jnp.where(outside, 0.0, jnp.where(even, own, other))
    pack(jnp.concatenate([first, jnp.zeros_like(own), last], axis=0), total)
    split(total, send_out, keep_out)


def finish_body(scale, mine_ref, other_ref, out_ref, total):
    channels = out_ref.shape[-1]
    half = mine_ref.shape[0]
    mine = half_of()
    total[pl.ds(pl.multiple_of(mine * half, 8), half)] = mine_ref[...] / scale
    total[pl.ds(pl.multiple_of((1 - mine) * half, 8), half)] = other_ref[...] / scale
    rows = 9 * channels // 4
    for ab in range(9):
        for c in range(3):
            first = ab * channels
            parts = []
            for r in range(first, first + channels, 8):
                if r < 3 * rows:
                    parts.append(total[r : r + 8, c * channels : (c + 1) * channels])
                else:
                    q = c * rows + r - 3 * rows
                    parts.append(total[q : q + 8, 3 * channels : 4 * channels])
            out_ref[ab // 3, ab % 3, c] = jnp.concatenate(parts, axis=0)


def inputs_body(cells_ref, far_ref, kernel_ref, out_ref, cells):
    channels, size_x, size_y, size_z = out_ref.shape
    ix = lax.axis_index("gx")
    cells[...] = cells_ref[...]

    @pl.when((ix != 0) & (ix != lax.axis_size("gx") - 1))
    def _():
        cells[jnp.where(ix % 2 == 0, 0, size_x + 1)] = far_ref[: size_y + 2]

    taps = jnp.concatenate(
        [
            jnp.concatenate([kernel_ref[a, b, c] for a in range(3) for b in range(3)], axis=0).astype(F32)
            for c in range(3)
        ],
        axis=1,
    )
    taps = jnp.transpose(taps).astype(BF16)
    for x in range(size_x):
        rows = []
        for y in range(0, size_y, 2):
            rhs = jnp.concatenate([stacked(cells, x, y), stacked(cells, x, y + 1)], axis=1)
            terms = jnp.dot(taps, rhs, preferred_element_type=F32)
            for k in range(2):
                part = terms[:, k * size_z : (k + 1) * size_z]
                row = shift_z(part[:channels], -1) + part[channels : 2 * channels]
                rows.append(row + shift_z(part[2 * channels :], 1))
        out_ref[:, x] = jnp.swapaxes(jnp.stack(rows), 0, 1).astype(BF16)


def shards(activation, out_grad, kernel):
    channels, size_x, size_y, size_z = activation.shape
    counts = (lax.axis_size("gx"), lax.axis_size("gy"))
    nx, ny = counts
    shape = jax.ShapeDtypeStruct
    volume = channels * size_x * size_y * size_z

    def permute(value, partner):
        return lax.ppermute(value, BOTH, pairs(counts, partner))

    def core(ix, iy):
        return ix ^ 1, iy

    def odd_x(ix, iy):
        return (ix + 1 if ix % 2 else ix - 1) % nx, iy

    def even_y(ix, iy):
        return ix, iy ^ 1

    def odd_y(ix, iy):
        if iy in (0, ny - 1):
            return ix ^ 1, iy
        return ix, (iy + 1 if iy % 2 else iy - 1)

    def call(name, body, out_shape, arrays, scratch=(), flops=0, in_specs=None, limit=16 << 20):
        outs = out_shape if isinstance(out_shape, tuple) else (out_shape,)
        nbytes = sum(a.size * a.dtype.itemsize for a in (*arrays, *outs))
        return pl.pallas_call(
            body,
            out_shape=out_shape,
            in_specs=in_specs or [VMEM] * len(arrays),
            out_specs=jax.tree.map(lambda _: VMEM, out_shape),
            scratch_shapes=list(scratch),
            compiler_params=params(limit),
            cost_estimate=cost(flops, nbytes),
            name=name,
        )(*arrays)

    grad, near = call(
        "gradient",
        gradient_body,
        (shape((size_x, size_y, channels, size_z), BF16), shape((size_y, channels, size_z), BF16)),
        (out_grad,),
        (
            pltpu.VMEM((size_x, channels, size_y, size_z), BF16),
            pltpu.SemaphoreType.DMA((size_x,)),
        ),
        in_specs=[pl.BlockSpec(memory_space=pltpu.HBM)],
        limit=16 << 20,
    )
    near = permute(near, core)
    face = shape((size_x + 1, channels, size_z), BF16)
    even, odd = call("faces", faces_body, (face, face), (grad, near))
    odd = permute(odd, odd_y)
    even = permute(even, even_y)
    act = call(
        "activation",
        activation_body,
        shape((size_x, size_y, 3 * channels, size_z), BF16),
        (activation,),
    )
    rows = (9 * 3 * channels * channels // 128 + 15) // 16 * 8
    half = shape((rows, 128), F32)
    whole = pltpu.VMEM((2 * rows, 128), F32)
    cells, far, send, total = call(
        "weights",
        weights_body,
        (
            shape((size_x + 2, size_y + 2, channels, size_z), BF16),
            shape((2 * size_y + 2, channels, size_z), BF16),
            half,
            half,
        ),
        (act, grad, near, even, odd),
        (whole,),
        flops=54 * channels * volume,
    )
    both = nx == 4
    if both:
        total = total + permute(send, core)
    far = permute(far, odd_x)
    across = functools.partial(across_body, both)
    far_send, far_total = call("across", across, (half, half), (act, cells, far), (whole,), flops=volume)
    if both:
        far_total = far_total + permute(far_send, core)
    else:
        total = total + far_total + permute(send + far_send, core)
    step = 2
    while step < nx:
        total = total + permute(total, lambda ix, iy: (ix ^ 1 ^ step, iy))
        step *= 2
    if both:
        total = total + far_total
    grad_input = call(
        "inputs",
        inputs_body,
        shape(activation.shape, BF16),
        (cells, far, kernel),
        (pltpu.VMEM(cells.shape, BF16),),
        flops=54 * channels * volume,
    )
    step = 1
    while step < ny:
        total = total + permute(total, lambda ix, iy: (ix ^ 1, iy ^ step))
        if step == 1:
            total, grad_input = lax.optimization_barrier((total, grad_input))
        step *= 2
    other = permute(total, core)
    cell_count = nx * size_x * ny * size_y * size_z
    finish = functools.partial(finish_body, float(cell_count) ** 0.5)
    grad_kernel = call("finish", finish, shape(kernel.shape, F32), (total, other), (whole,))
    return (grad_input, grad_kernel)


def solution(mesh):
    return jax.shard_map(
        shards,
        mesh=mesh,
        in_specs=(P(None, "gx", "gy", None), P(None, "gx", "gy", None), P()),
        out_specs=(P(None, "gx", "gy", None), P()),
        check_vma=False,
    )
```

```python
import functools

import jax
import jax.numpy as jnp
from jax import lax
from jax.experimental import pallas as pl
from jax.experimental.pallas import tpu as pltpu
from jax.sharding import PartitionSpec as P

BOTH = ("gx", "gy")
VMEM = pl.BlockSpec(memory_space=pltpu.VMEM)
BF16, F32 = jnp.bfloat16, jnp.float32


def params(limit=16 << 20):
    return pltpu.CompilerParams(vmem_limit_bytes=limit)


def cost(flops, nbytes):
    return pl.CostEstimate(flops=flops, bytes_accessed=nbytes, transcendentals=0)


def pairs(counts, partner):
    nx, ny = counts
    flat = []
    for ix in range(nx):
        for iy in range(ny):
            jx, jy = partner(ix, iy)
            flat.append((ix * ny + iy, jx * ny + jy))
    return flat


def shift_z(cells, step):
    size = cells.shape[-1]
    lane = lax.broadcasted_iota(jnp.int32, cells.shape, cells.ndim - 1)
    moved = pltpu.roll(cells, step % size, cells.ndim - 1)
    return jnp.where(lane == (0 if step == 1 else size - 1), 0.0, moved)


def gradient_body(grad_hbm, grad_out, near_out, held, sems):
    size_x = grad_out.shape[0]
    copies = [pltpu.make_async_copy(grad_hbm.at[:, x], held.at[x], sems.at[x]) for x in range(size_x)]
    for copy in copies:
        copy.start()
    for x, copy in enumerate(copies):
        copy.wait()
        grad_out[x] = jnp.swapaxes(held[x].astype(F32), 0, 1).astype(BF16)
    near_out[...] = grad_out[jnp.where(lax.axis_index("gx") % 2 == 0, size_x - 1, 0)]


def activation_body(act_ref, act_out):
    channels, size_x = act_ref.shape[:2]
    for x in range(size_x):
        act = jnp.swapaxes(act_ref[:, x].astype(F32), 0, 1)
        act_out[x, :, :channels] = shift_z(act, 1).astype(BF16)
        act_out[x, :, channels : 2 * channels] = act.astype(BF16)
        act_out[x, :, 2 * channels :] = shift_z(act, -1).astype(BF16)


def faces_body(grad_ref, near_ref, even_out, odd_out):
    size_x, size_y = grad_ref.shape[:2]
    high = jnp.where(lax.axis_index("gy") % 2 == 0, size_y - 1, 0)
    for out, y in ((even_out, high), (odd_out, size_y - 1 - high)):
        for x in range(size_x):
            out[x] = grad_ref[x, y]
        out[size_x] = near_ref[y]


def half_of():
    bits = lax.axis_index("gx") ^ lax.axis_index("gy")
    width = max(lax.axis_size("gx"), lax.axis_size("gy")).bit_length()
    parity = bits & 1
    for k in range(1, width):
        parity = parity ^ ((bits >> k) & 1)
    return parity


def stacked(cells, x, y):
    return jnp.concatenate([cells[x - a + 2, y - b + 2] for a in range(3) for b in range(3)], axis=0)


def pack_half(terms, half, out):
    channels = terms.shape[1] // 3
    part = channels // 2
    count = out.shape[0] // part

    def rows(slot):
        return pl.ds(pl.multiple_of(slot * channels + half * part, 8), part)

    for k in range(count):
        main = terms[rows(k)]
        slot, c = divmod(k, 3)
        if count + slot < 9:
            side = terms[rows(count + slot)][:, c * channels : (c + 1) * channels]
        else:
            side = jnp.zeros((part, channels), F32)
        out[k * part : (k + 1) * part] = jnp.concatenate([main, side], axis=1)


def split(terms, send_out, keep_out):
    mine = half_of()
    pack_half(terms, mine, keep_out)
    pack_half(terms, 1 - mine, send_out)


def outer(lhs, rhs):
    dims = (((1,), (1,)), ((), ()))
    total = None
    for k in range(0, len(lhs), 2):
        term = lax.dot_general(
            jnp.concatenate(lhs[k : k + 2], axis=1),
            jnp.concatenate(rhs[k : k + 2], axis=1),
            dims,
            preferred_element_type=F32,
        )
        total = term if total is None else total + term
    return total


def inner_body(act_ref, grad_ref, near_ref, cells, acc_out):
    size_x, size_y, rows3, size_z = act_ref.shape
    even = lax.axis_index("gx") % 2 == 0
    near = jnp.where(even, size_x + 1, 0)
    zero = jnp.zeros((rows3 // 3, size_z), BF16)
    for y in range(size_y + 2):
        inside = 0 < y <= size_y
        cells[near, y] = near_ref[y - 1] if inside else zero
        cells[size_x + 1 - near, y] = zero
        for x in range(size_x):
            cells[x + 1, y] = grad_ref[x, y - 1] if inside else zero
    order = [(x, y) for x in range(size_x) for y in range(size_y)]
    acc_out[...] = outer([stacked(cells, x, y) for x, y in order], [act_ref[x, y] for x, y in order])


def edges_body(act_ref, inner_ref, acc_ref, even_ref, odd_ref, cells, far_out, send_out, keep_out, acc):
    size_x, size_y, rows3, size_z = act_ref.shape
    channels = rows3 // 3
    ix, iy = lax.axis_index("gx"), lax.axis_index("gy")
    near = jnp.where(ix % 2 == 0, size_x + 1, 0)
    zero = jnp.zeros((channels, size_z), BF16)
    cells[...] = inner_ref[...]
    for x in range(size_x + 1):
        at = x + 1 if x < size_x else near
        low = jnp.where(iy % 2 == 0, odd_ref[x], even_ref[x])
        high = jnp.where(iy % 2 == 0, even_ref[x], odd_ref[x])
        cells[at, 0] = jnp.where(iy == 0, zero, low)
        cells[at, size_y + 1] = jnp.where(iy == lax.axis_size("gy") - 1, zero, high)
    edge = jnp.where(ix % 2 == 0, 0, size_x - 1)
    far_out[: size_y + 2] = cells[edge + 1]
    for y in range(size_y):
        far_out[size_y + 2 + y] = act_ref[edge, y, channels : 2 * channels]
    acc[...] = acc_ref[...]
    for b, row, y in ((2, 0, 0), (0, size_y + 1, size_y - 1)):
        lhs = [jnp.concatenate([cells[x - a + 2, row] for a in range(3)], axis=0) for x in range(size_x)]
        terms = outer(lhs, [act_ref[x, y] for x in range(size_x)])
        for a in range(3):
            first = (3 * a + b) * channels
            acc[first : first + channels] += terms[a * channels : (a + 1) * channels]
    split(acc, send_out, keep_out)


def across_body(both, act_ref, cells, far_ref, send_out, keep_out, acc):
    size_x, size_y, rows3, size_z = act_ref.shape
    channels = rows3 // 3
    ix = lax.axis_index("gx")
    even = ix % 2 == 0
    edge = jnp.where(even, 0, size_x - 1)

    def product(grads, acts):
        lhs = [jnp.concatenate([grads(y - b + 2) for b in range(3)], axis=0) for y in range(size_y)]
        return outer(lhs, [acts(y) for y in range(size_y)])

    def offsets(y):
        act = far_ref[size_y + 2 + y].astype(F32)
        return jnp.concatenate([shift_z(act, 1), act, shift_z(act, -1)], axis=0).astype(BF16)

    own = product(lambda y: far_ref[y], lambda y: act_ref[edge, y])
    other = product(lambda y: cells[edge + 1, y], offsets) if both else jnp.zeros_like(own)
    outside = (ix == 0) | (ix == lax.axis_size("gx") - 1)
    rows = 3 * channels
    acc[:rows] = jnp.where(outside, 0.0, jnp.where(even, other, own))
    acc[rows : 2 * rows] = jnp.zeros_like(own)
    acc[2 * rows :] = jnp.where(outside, 0.0, jnp.where(even, own, other))
    split(acc, send_out, keep_out)


def finish_body(scale, half_ref, *refs):
    out_ref = refs[-1]
    part, channels = out_ref.shape[-2:]
    count = half_ref.shape[0] // part
    for k in range(count):
        rows = half_ref[k * part : (k + 1) * part] / scale
        for c in range(3):
            out_ref[k // 3, k % 3, c] = rows[:, c * channels : (c + 1) * channels]
        slot, c = divmod(k, 3)
        if count + slot < 9:
            out_ref[(count + slot) // 3, (count + slot) % 3, c] = rows[:, 3 * channels :]


def inputs_body(cells_ref, far_ref, kernel_ref, out_ref, cells):
    channels, size_x, size_y, size_z = out_ref.shape
    ix = lax.axis_index("gx")
    cells[...] = cells_ref[...]

    @pl.when((ix != 0) & (ix != lax.axis_size("gx") - 1))
    def _():
        cells[jnp.where(ix % 2 == 0, 0, size_x + 1)] = far_ref[: size_y + 2]

    taps = jnp.concatenate(
        [
            jnp.concatenate([kernel_ref[a, b, c] for a in range(3) for b in range(3)], axis=0).astype(F32)
            for c in range(3)
        ],
        axis=1,
    )
    taps = jnp.transpose(taps).astype(BF16)
    for x in range(size_x):
        rows = []
        for y in range(0, size_y, 2):
            rhs = jnp.concatenate([stacked(cells, x, y), stacked(cells, x, y + 1)], axis=1)
            terms = jnp.dot(taps, rhs, preferred_element_type=F32)
            for k in range(2):
                part = terms[:, k * size_z : (k + 1) * size_z]
                row = shift_z(part[:channels], -1) + part[channels : 2 * channels]
                rows.append(row + shift_z(part[2 * channels :], 1))
        out_ref[:, x] = jnp.swapaxes(jnp.stack(rows), 0, 1).astype(BF16)


def shards(activation, out_grad, kernel):
    channels, size_x, size_y, size_z = activation.shape
    counts = (lax.axis_size("gx"), lax.axis_size("gy"))
    nx, ny = counts
    shape = jax.ShapeDtypeStruct
    volume = channels * size_x * size_y * size_z

    def permute(value, partner):
        return lax.ppermute(value, BOTH, pairs(counts, partner))

    def core(ix, iy):
        return ix ^ 1, iy

    def odd_x(ix, iy):
        return (ix + 1 if ix % 2 else ix - 1) % nx, iy

    def even_y(ix, iy):
        return ix, iy ^ 1

    def odd_y(ix, iy):
        if iy in (0, ny - 1):
            return ix ^ 1, iy
        return ix, (iy + 1 if iy % 2 else iy - 1)

    def call(name, body, out_shape, arrays, scratch=(), flops=0, in_specs=None, limit=16 << 20):
        outs = out_shape if isinstance(out_shape, tuple) else (out_shape,)
        nbytes = sum(a.size * a.dtype.itemsize for a in (*arrays, *outs))
        return pl.pallas_call(
            body,
            out_shape=out_shape,
            in_specs=in_specs or [VMEM] * len(arrays),
            out_specs=jax.tree.map(lambda _: VMEM, out_shape),
            scratch_shapes=list(scratch),
            compiler_params=params(limit),
            cost_estimate=cost(flops, nbytes),
            name=name,
        )(*arrays)

    grad, near = call(
        "gradient",
        gradient_body,
        (shape((size_x, size_y, channels, size_z), BF16), shape((size_y, channels, size_z), BF16)),
        (out_grad,),
        (
            pltpu.VMEM((size_x, channels, size_y, size_z), BF16),
            pltpu.SemaphoreType.DMA((size_x,)),
        ),
        in_specs=[pl.BlockSpec(memory_space=pltpu.HBM)],
        limit=16 << 20,
    )
    near = permute(near, core)
    face = shape((size_x + 1, channels, size_z), BF16)
    even, odd = call("faces", faces_body, (face, face), (grad, near))
    odd = permute(odd, odd_y)
    even = permute(even, even_y)
    act = call(
        "activation",
        activation_body,
        shape((size_x, size_y, 3 * channels, size_z), BF16),
        (activation,),
    )
    cells_shape = shape((size_x + 2, size_y + 2, channels, size_z), BF16)
    terms = shape((9 * channels, 3 * channels), F32)
    half = shape((7 * channels // 2, 4 * channels), F32)
    acc = pltpu.VMEM(terms.shape, F32)
    cells, inner = call(
        "inner",
        inner_body,
        (cells_shape, terms),
        (act, grad, near),
        flops=54 * channels * volume,
    )
    cells, far, send, total = call(
        "edges",
        edges_body,
        (cells_shape, shape((2 * size_y + 2, channels, size_z), BF16), half, half),
        (act, cells, inner, even, odd),
        (acc,),
        flops=12 * channels * volume,
    )
    both = nx == 4
    if both:
        total = total + permute(send, core)
    far = permute(far, odd_x)
    across = functools.partial(across_body, both)
    far_send, far_total = call("across", across, (half, half), (act, cells, far), (acc,), flops=volume)
    if both:
        far_total = far_total + permute(far_send, core)
    else:
        total = total + far_total + permute(send + far_send, core)
    step = 2
    while step < nx:
        total = total + permute(total, lambda ix, iy: (ix ^ 1 ^ step, iy))
        step *= 2
    if both:
        total = total + far_total
    grad_input = call(
        "inputs",
        inputs_body,
        shape(activation.shape, BF16),
        (cells, far, kernel),
        (pltpu.VMEM(cells.shape, BF16),),
        flops=54 * channels * volume,
    )
    step = 1
    while step < ny:
        total = total + permute(total, lambda ix, iy: (ix ^ 1, iy ^ step))
        if step == 1:
            total, grad_input = lax.optimization_barrier((total, grad_input))
        step *= 2
    other = permute(total, core)
    cell_count = nx * size_x * ny * size_y * size_z
    finish = functools.partial(finish_body, float(cell_count) ** 0.5)

    def finished(value, mine, *before):
        return pl.pallas_call(
            finish,
            out_shape=shape(kernel.shape, F32),
            grid=(1,),
            in_specs=[VMEM] + [pl.BlockSpec(memory_space=pl.ANY)] * len(before),
            out_specs=pl.BlockSpec(
                (3, 3, 3, channels // 2, channels),
                lambda i: (0, 0, 0, half_of() if mine else 1 - half_of(), 0),
            ),
            input_output_aliases={1: 0} if before else {},
            compiler_params=params(),
            cost_estimate=cost(0, 8 * value.size),
            name="finish",
        )(value, *before)

    grad_kernel = finished(other, False, finished(total, True))
    return (grad_input, grad_kernel)


def solution(mesh):
    return jax.shard_map(
        shards,
        mesh=mesh,
        in_specs=(P(None, "gx", "gy", None), P(None, "gx", "gy", None), P()),
        out_specs=(P(None, "gx", "gy", None), P()),
        check_vma=False,
    )
```

```python
import functools

import jax
import jax.numpy as jnp
from jax import lax
from jax.experimental import pallas as pl
from jax.experimental.pallas import tpu as pltpu
from jax.sharding import PartitionSpec as P


BOTH = ("gx", "gy")
VMEM = pl.BlockSpec(memory_space=pltpu.VMEM)
BF16, F32 = jnp.bfloat16, jnp.float32


def params(limit=16 << 20):
    return pltpu.CompilerParams(vmem_limit_bytes=limit)


def cost(flops, nbytes):
    return pl.CostEstimate(flops=flops, bytes_accessed=nbytes, transcendentals=0)


def pairs(counts, partner):
    nx, ny = counts
    flat = []
    for ix in range(nx):
        for iy in range(ny):
            jx, jy = partner(ix, iy)
            flat.append((ix * ny + iy, jx * ny + jy))
    return flat


def shift_z(cells, step):
    size = cells.shape[-1]
    lane = lax.broadcasted_iota(jnp.int32, cells.shape, cells.ndim - 1)
    moved = pltpu.roll(cells, step % size, cells.ndim - 1)
    return jnp.where(lane == (0 if step == 1 else size - 1), 0.0, moved)


def gradient_body(grad_hbm, grad_out, near_out, held, sems):
    size_x = grad_out.shape[0]
    copies = [pltpu.make_async_copy(grad_hbm.at[:, x], held.at[x], sems.at[x]) for x in range(size_x)]
    for copy in copies:
        copy.start()
    for x, copy in enumerate(copies):
        copy.wait()
        grad_out[x] = jnp.swapaxes(held[x].astype(F32), 0, 1).astype(BF16)
    near_out[...] = grad_out[jnp.where(lax.axis_index("gx") % 2 == 0, size_x - 1, 0)]


def activation_body(act_ref, act_out):
    channels, size_x = act_ref.shape[:2]
    for x in range(size_x):
        act = jnp.swapaxes(act_ref[:, x].astype(F32), 0, 1)
        act_out[x, :, :channels] = shift_z(act, 1).astype(BF16)
        act_out[x, :, channels : 2 * channels] = act.astype(BF16)
        act_out[x, :, 2 * channels :] = shift_z(act, -1).astype(BF16)


def faces_body(grad_ref, near_ref, even_out, odd_out):
    size_x, size_y = grad_ref.shape[:2]
    high = jnp.where(lax.axis_index("gy") % 2 == 0, size_y - 1, 0)
    for out, y in ((even_out, high), (odd_out, size_y - 1 - high)):
        for x in range(size_x):
            out[x] = grad_ref[x, y]
        out[size_x] = near_ref[y]


def half_of():
    bits = lax.axis_index("gx") ^ lax.axis_index("gy")
    width = max(lax.axis_size("gx"), lax.axis_size("gy")).bit_length()
    parity = bits & 1
    for k in range(1, width):
        parity = parity ^ ((bits >> k) & 1)
    return parity


def stacked(cells, x, y):
    return jnp.concatenate([cells[x - a + 2, y - b + 2] for a in range(3) for b in range(3)], axis=0)


def pack_half(terms, half, out):
    channels = terms.shape[1] // 3
    part = channels // 2
    count = out.shape[0] // part

    def rows(slot):
        return pl.ds(pl.multiple_of(slot * channels + half * part, 8), part)

    for k in range(count):
        main = terms[rows(k)]
        slot, c = divmod(k, 3)
        if count + slot < 9:
            side = terms[rows(count + slot)][:, c * channels : (c + 1) * channels]
        else:
            side = jnp.zeros((part, channels), F32)
        out[k * part : (k + 1) * part] = jnp.concatenate([main, side], axis=1)


def split(terms, send_out, keep_out):
    mine = half_of()
    pack_half(terms, mine, keep_out)
    pack_half(terms, 1 - mine, send_out)


def outer(lhs, rhs):
    dims = (((1,), (1,)), ((), ()))
    total = None
    for k in range(0, len(lhs), 2):
        term = lax.dot_general(
            jnp.concatenate(lhs[k : k + 2], axis=1),
            jnp.concatenate(rhs[k : k + 2], axis=1),
            dims,
            preferred_element_type=F32,
        )
        total = term if total is None else total + term
    return total


def inner_body(act_ref, grad_ref, near_ref, cells, acc_out):
    size_x, size_y, rows3, size_z = act_ref.shape
    even = lax.axis_index("gx") % 2 == 0
    near = jnp.where(even, size_x + 1, 0)
    zero = jnp.zeros((rows3 // 3, size_z), BF16)
    for y in range(size_y + 2):
        inside = 0 < y <= size_y
        cells[near, y] = near_ref[y - 1] if inside else zero
        cells[size_x + 1 - near, y] = zero
        for x in range(size_x):
            cells[x + 1, y] = grad_ref[x, y - 1] if inside else zero
    order = [(x, y) for x in range(size_x) for y in range(size_y)]
    acc_out[...] = outer([stacked(cells, x, y) for x, y in order], [act_ref[x, y] for x, y in order])


def edges_body(act_ref, inner_ref, acc_ref, even_ref, odd_ref, cells, far_out, send_out, keep_out, acc):
    size_x, size_y, rows3, size_z = act_ref.shape
    channels = rows3 // 3
    ix, iy = lax.axis_index("gx"), lax.axis_index("gy")
    near = jnp.where(ix % 2 == 0, size_x + 1, 0)
    zero = jnp.zeros((channels, size_z), BF16)
    cells[...] = inner_ref[...]
    for x in range(size_x + 1):
        at = x + 1 if x < size_x else near
        low = jnp.where(iy % 2 == 0, odd_ref[x], even_ref[x])
        high = jnp.where(iy % 2 == 0, even_ref[x], odd_ref[x])
        cells[at, 0] = jnp.where(iy == 0, zero, low)
        cells[at, size_y + 1] = jnp.where(iy == lax.axis_size("gy") - 1, zero, high)
    edge = jnp.where(ix % 2 == 0, 0, size_x - 1)
    far_out[: size_y + 2] = cells[edge + 1]
    for y in range(size_y):
        far_out[size_y + 2 + y] = act_ref[edge, y, channels : 2 * channels]
    acc[...] = acc_ref[...]
    for b, row, y in ((2, 0, 0), (0, size_y + 1, size_y - 1)):
        lhs = [jnp.concatenate([cells[x - a + 2, row] for a in range(3)], axis=0) for x in range(size_x)]
        terms = outer(lhs, [act_ref[x, y] for x in range(size_x)])
        for a in range(3):
            first = (3 * a + b) * channels
            acc[first : first + channels] += terms[a * channels : (a + 1) * channels]
    split(acc, send_out, keep_out)


def across_body(both, act_ref, cells, far_ref, send_out, keep_out, acc):
    size_x, size_y, rows3, _ = act_ref.shape
    channels = rows3 // 3
    ix = lax.axis_index("gx")
    even = ix % 2 == 0
    edge = jnp.where(even, 0, size_x - 1)

    def product(grads, acts):
        lhs = [jnp.concatenate([grads(y - b + 2) for b in range(3)], axis=0) for y in range(size_y)]
        return outer(lhs, [acts(y) for y in range(size_y)])

    def offsets(y):
        act = far_ref[size_y + 2 + y].astype(F32)
        return jnp.concatenate([shift_z(act, 1), act, shift_z(act, -1)], axis=0).astype(BF16)

    own = product(lambda y: far_ref[y], lambda y: act_ref[edge, y])
    other = product(lambda y: cells[edge + 1, y], offsets) if both else jnp.zeros_like(own)
    outside = (ix == 0) | (ix == lax.axis_size("gx") - 1)
    rows = 3 * channels
    acc[:rows] = jnp.where(outside, 0.0, jnp.where(even, other, own))
    acc[rows : 2 * rows] = jnp.zeros_like(own)
    acc[2 * rows :] = jnp.where(outside, 0.0, jnp.where(even, own, other))
    split(acc, send_out, keep_out)


def finish_body(scale, half_ref, *refs):
    out_ref = refs[-1]
    part, channels = out_ref.shape[-2:]
    count = half_ref.shape[0] // part
    for k in range(count):
        rows = half_ref[k * part : (k + 1) * part] / scale
        for c in range(3):
            out_ref[k // 3, k % 3, c] = rows[:, c * channels : (c + 1) * channels]
        slot, c = divmod(k, 3)
        if count + slot < 9:
            out_ref[(count + slot) // 3, (count + slot) % 3, c] = rows[:, 3 * channels :]


def inputs_body(cells_ref, far_ref, kernel_ref, out_ref, cells):
    channels, size_x, size_y, size_z = out_ref.shape
    ix = lax.axis_index("gx")
    cells[...] = cells_ref[...]

    @pl.when((ix != 0) & (ix != lax.axis_size("gx") - 1))
    def _():
        cells[jnp.where(ix % 2 == 0, 0, size_x + 1)] = far_ref[: size_y + 2]

    taps = jnp.concatenate(
        [
            jnp.concatenate([kernel_ref[a, b, c] for a in range(3) for b in range(3)], axis=0).astype(F32)
            for c in range(3)
        ],
        axis=1,
    )
    taps = jnp.transpose(taps).astype(BF16)
    for x in range(size_x):
        rows = []
        for y in range(0, size_y, 2):
            rhs = jnp.concatenate([stacked(cells, x, y), stacked(cells, x, y + 1)], axis=1)
            terms = jnp.dot(taps, rhs, preferred_element_type=F32)
            for k in range(2):
                part = terms[:, k * size_z : (k + 1) * size_z]
                row = shift_z(part[:channels], -1) + part[channels : 2 * channels]
                rows.append(row + shift_z(part[2 * channels :], 1))
        out_ref[:, x] = jnp.swapaxes(jnp.stack(rows), 0, 1).astype(BF16)


def shards(activation, out_grad, kernel):
    channels, size_x, size_y, size_z = activation.shape
    counts = (lax.axis_size("gx"), lax.axis_size("gy"))
    nx, ny = counts
    shape = jax.ShapeDtypeStruct
    volume = channels * size_x * size_y * size_z

    def permute(value, partner):
        return lax.ppermute(value, BOTH, pairs(counts, partner))

    def core(ix, iy):
        return ix ^ 1, iy

    def odd_x(ix, iy):
        return (ix + 1 if ix % 2 else ix - 1) % nx, iy

    def even_y(ix, iy):
        return ix, iy ^ 1

    def odd_y(ix, iy):
        if iy in (0, ny - 1):
            return ix ^ 1, iy
        return ix, (iy + 1 if iy % 2 else iy - 1)

    def call(body, out_shape, arrays, scratch=(), flops=0, in_specs=None, limit=16 << 20):
        outs = out_shape if isinstance(out_shape, tuple) else (out_shape,)
        nbytes = sum(a.size * a.dtype.itemsize for a in (*arrays, *outs))
        return pl.pallas_call(
            body,
            out_shape=out_shape,
            in_specs=in_specs or [VMEM] * len(arrays),
            out_specs=jax.tree.map(lambda _: VMEM, out_shape),
            scratch_shapes=list(scratch),
            compiler_params=params(limit),
            cost_estimate=cost(flops, nbytes),
        )(*arrays)

    grad, near = call(
        gradient_body,
        (shape((size_x, size_y, channels, size_z), BF16), shape((size_y, channels, size_z), BF16)),
        (out_grad,),
        (
            pltpu.VMEM((size_x, channels, size_y, size_z), BF16),
            pltpu.SemaphoreType.DMA((size_x,)),
        ),
        in_specs=[pl.BlockSpec(memory_space=pltpu.HBM)],
        limit=16 << 20,
    )
    near = permute(near, core)
    face = shape((size_x + 1, channels, size_z), BF16)
    even, odd = call(faces_body, (face, face), (grad, near))
    odd = permute(odd, odd_y)
    even = permute(even, even_y)
    act = call(activation_body, shape((size_x, size_y, 3 * channels, size_z), BF16), (activation,))
    cells_shape = shape((size_x + 2, size_y + 2, channels, size_z), BF16)
    terms = shape((9 * channels, 3 * channels), F32)
    half = shape((7 * channels // 2, 4 * channels), F32)
    acc = pltpu.VMEM(terms.shape, F32)
    cells, inner = call(inner_body, (cells_shape, terms), (act, grad, near), flops=54 * channels * volume)
    cells, far, send, total = call(
        edges_body,
        (cells_shape, shape((2 * size_y + 2, channels, size_z), BF16), half, half),
        (act, cells, inner, even, odd),
        (acc,),
        flops=12 * channels * volume,
    )
    both = nx == 4
    if both:
        total = total + permute(send, core)
    far = permute(far, odd_x)
    across = functools.partial(across_body, both)
    far_send, far_total = call(across, (half, half), (act, cells, far), (acc,), flops=volume)
    if both:
        far_total = far_total + permute(far_send, core)
    else:
        total = total + far_total + permute(send + far_send, core)
    step = 2
    while step < nx:
        total = total + permute(total, lambda ix, iy: (ix ^ 1 ^ step, iy))
        step *= 2
    if both:
        total = total + far_total
    grad_input = call(
        inputs_body,
        shape(activation.shape, BF16),
        (cells, far, kernel),
        (pltpu.VMEM(cells.shape, BF16),),
        flops=54 * channels * volume,
    )
    step = 1
    while step < ny:
        total = total + permute(total, lambda ix, iy: (ix ^ 1, iy ^ step))
        if step == 1:
            total, grad_input = lax.optimization_barrier((total, grad_input))
        step *= 2
    other = permute(total, core)
    cell_count = nx * size_x * ny * size_y * size_z
    finish = functools.partial(finish_body, float(cell_count) ** 0.5)

    def finished(value, mine, *before):
        return pl.pallas_call(
            finish,
            out_shape=shape(kernel.shape, F32),
            grid=(1,),
            in_specs=[VMEM] + [pl.BlockSpec(memory_space=pl.ANY)] * len(before),
            out_specs=pl.BlockSpec(
                (3, 3, 3, channels // 2, channels),
                lambda i: (0, 0, 0, half_of() if mine else 1 - half_of(), 0),
            ),
            input_output_aliases={1: 0} if before else {},
            compiler_params=params(),
            cost_estimate=cost(0, 8 * value.size),
            name="finish",
        )(value, *before)

    grad_kernel = finished(other, False, finished(total, True))
    return (grad_input, grad_kernel)


def solution(mesh):
    return jax.shard_map(
        shards,
        mesh=mesh,
        in_specs=(P(None, "gx", "gy", None), P(None, "gx", "gy", None), P()),
        out_specs=(P(None, "gx", "gy", None), P()),
        check_vma=False,
    )
```

```python
import functools

import jax
import jax.numpy as jnp
from jax import lax
from jax.experimental import pallas as pl
from jax.experimental.pallas import tpu as pltpu
from jax.sharding import PartitionSpec as P


BOTH = ("gx", "gy")
VMEM = pl.BlockSpec(memory_space=pltpu.VMEM)
BF16, F32 = jnp.bfloat16, jnp.float32


def params(limit=16 << 20):
    return pltpu.CompilerParams(vmem_limit_bytes=limit)


def cost(flops, nbytes):
    return pl.CostEstimate(flops=flops, bytes_accessed=nbytes, transcendentals=0)


def pairs(counts, partner):
    nx, ny = counts
    flat = []
    for ix in range(nx):
        for iy in range(ny):
            jx, jy = partner(ix, iy)
            flat.append((ix * ny + iy, jx * ny + jy))
    return flat


def shift_z(cells, step):
    size = cells.shape[-1]
    lane = lax.broadcasted_iota(jnp.int32, cells.shape, cells.ndim - 1)
    moved = pltpu.roll(cells, step % size, cells.ndim - 1)
    return jnp.where(lane == (0 if step == 1 else size - 1), 0.0, moved)


def gradient_body(grad_ref, grad_out, even_out, odd_out):
    size_x, size_y = grad_out.shape[:2]
    for x in range(size_x):
        grad_out[x] = jnp.swapaxes(grad_ref[:, x].astype(F32), 0, 1).astype(BF16)
    high = jnp.where(lax.axis_index("gy") % 2 == 0, size_y - 1, 0)
    for x in range(size_x):
        even_out[x] = grad_out[x, high]
        odd_out[x] = grad_out[x, size_y - 1 - high]


def activation_body(act_ref, act_out):
    channels, size_x = act_ref.shape[:2]
    for x in range(size_x):
        act = jnp.swapaxes(act_ref[:, x].astype(F32), 0, 1)
        act_out[x, :, :channels] = shift_z(act, 1).astype(BF16)
        act_out[x, :, channels : 2 * channels] = act.astype(BF16)
        act_out[x, :, 2 * channels :] = shift_z(act, -1).astype(BF16)


def half_of():
    bits = lax.axis_index("gx") ^ lax.axis_index("gy")
    width = max(lax.axis_size("gx"), lax.axis_size("gy")).bit_length()
    parity = bits & 1
    for k in range(1, width):
        parity = parity ^ ((bits >> k) & 1)
    return parity


def stacked(cells, x, y):
    return jnp.concatenate([cells[x - a + 2, y - b + 2] for a in range(3) for b in range(3)], axis=0)


def pack_half(terms, half, out):
    channels = terms.shape[1] // 3
    part = channels // 2
    count = out.shape[0] // part

    def rows(slot):
        return pl.ds(pl.multiple_of(slot * channels + half * part, 8), part)

    for k in range(count):
        main = terms[rows(k)]
        slot, c = divmod(k, 3)
        if count + slot < 9:
            side = terms[rows(count + slot)][:, c * channels : (c + 1) * channels]
        else:
            side = jnp.zeros((part, channels), F32)
        out[k * part : (k + 1) * part] = jnp.concatenate([main, side], axis=1)


def split(terms, send_out, keep_out):
    mine = half_of()
    pack_half(terms, mine, keep_out)
    pack_half(terms, 1 - mine, send_out)


def outer(lhs, rhs):
    dims = (((1,), (1,)), ((), ()))
    total = None
    for k in range(0, len(lhs), 2):
        term = lax.dot_general(
            jnp.concatenate(lhs[k : k + 2], axis=1),
            jnp.concatenate(rhs[k : k + 2], axis=1),
            dims,
            preferred_element_type=F32,
        )
        total = term if total is None else total + term
    return total


def inner_body(act_ref, grad_ref, cells, acc_out):
    size_x, size_y, rows3, size_z = act_ref.shape
    zero = jnp.zeros((rows3 // 3, size_z), BF16)
    for x in range(size_x + 2):
        for y in range(size_y + 2):
            inside = 0 < x <= size_x and 0 < y <= size_y
            cells[x, y] = grad_ref[x - 1, y - 1] if inside else zero
    order = [(x, y) for x in range(size_x) for y in range(size_y)]
    acc_out[...] = outer([stacked(cells, x, y) for x, y in order], [act_ref[x, y] for x, y in order])


def edges_body(act_ref, inner_ref, acc_ref, even_ref, odd_ref, cells, near_out, far_out, send_out, keep_out, acc):
    size_x, size_y, rows3, size_z = act_ref.shape
    channels = rows3 // 3
    even, iy = lax.axis_index("gx") % 2 == 0, lax.axis_index("gy")
    zero = jnp.zeros((channels, size_z), BF16)
    cells[...] = inner_ref[...]
    for x in range(size_x):
        low = jnp.where(iy % 2 == 0, odd_ref[x], even_ref[x])
        high = jnp.where(iy % 2 == 0, even_ref[x], odd_ref[x])
        cells[x + 1, 0] = jnp.where(iy == 0, zero, low)
        cells[x + 1, size_y + 1] = jnp.where(iy == lax.axis_size("gy") - 1, zero, high)
    for out, edge in ((near_out, jnp.where(even, size_x - 1, 0)), (far_out, jnp.where(even, 0, size_x - 1))):
        out[: size_y + 2] = cells[edge + 1]
        for y in range(size_y):
            out[size_y + 2 + y] = act_ref[edge, y, channels : 2 * channels]
    acc[...] = acc_ref[...]
    for b, row, y in ((2, 0, 0), (0, size_y + 1, size_y - 1)):
        lhs = [jnp.concatenate([cells[x - a + 2, row] for a in range(3)], axis=0) for x in range(size_x)]
        terms = outer(lhs, [act_ref[x, y] for x in range(size_x)])
        for a in range(3):
            first = (3 * a + b) * channels
            acc[first : first + channels] += terms[a * channels : (a + 1) * channels]
    split(acc, send_out, keep_out)


def across(right, both, act_ref, cells, side_ref, acc):
    size_x, size_y, rows3, _ = act_ref.shape
    channels = rows3 // 3
    edge = jnp.where(right, size_x - 1, 0)

    def product(grads, acts):
        lhs = [jnp.concatenate([grads(y - b + 2) for b in range(3)], axis=0) for y in range(size_y)]
        return outer(lhs, [acts(y) for y in range(size_y)])

    def offsets(y):
        act = side_ref[size_y + 2 + y].astype(F32)
        return jnp.concatenate([shift_z(act, 1), act, shift_z(act, -1)], axis=0).astype(BF16)

    own = product(lambda y: side_ref[y], lambda y: act_ref[edge, y])
    other = product(lambda y: cells[edge + 1, y], offsets) if both else jnp.zeros_like(own)
    rows = 3 * channels
    acc[:rows] = jnp.where(right, own, other)
    acc[rows : 2 * rows] = jnp.zeros_like(own)
    acc[2 * rows :] = jnp.where(right, other, own)


def near_body(act_ref, cells, near_ref, keep_ref, half_ref, total_out, acc):
    across(lax.axis_index("gx") % 2 == 0, True, act_ref, cells, near_ref, acc)
    pack_half(acc, half_of(), total_out)
    total_out[...] += keep_ref[...] + half_ref[...]


def far_body(both, act_ref, cells, far_ref, send_out, keep_out, acc):
    ix = lax.axis_index("gx")
    across(ix % 2 == 1, both, act_ref, cells, far_ref, acc)

    @pl.when((ix == 0) | (ix == lax.axis_size("gx") - 1))
    def _():
        acc[...] = jnp.zeros_like(acc)

    split(acc, send_out, keep_out)


def finish_body(scale, half_ref, *refs):
    out_ref = refs[-1]
    part, channels = out_ref.shape[-2:]
    count = half_ref.shape[0] // part
    for k in range(count):
        rows = half_ref[k * part : (k + 1) * part] / scale
        for c in range(3):
            out_ref[k // 3, k % 3, c] = rows[:, c * channels : (c + 1) * channels]
        slot, c = divmod(k, 3)
        if count + slot < 9:
            out_ref[(count + slot) // 3, (count + slot) % 3, c] = rows[:, 3 * channels :]


def inputs_body(cells_ref, near_ref, far_ref, kernel_ref, out_ref, cells):
    channels, size_x, size_y, size_z = out_ref.shape
    ix = lax.axis_index("gx")
    cells[...] = cells_ref[...]
    cells[jnp.where(ix % 2 == 0, size_x + 1, 0)] = near_ref[: size_y + 2]

    @pl.when((ix != 0) & (ix != lax.axis_size("gx") - 1))
    def _():
        cells[jnp.where(ix % 2 == 0, 0, size_x + 1)] = far_ref[: size_y + 2]

    taps = jnp.concatenate(
        [
            jnp.concatenate([kernel_ref[a, b, c] for a in range(3) for b in range(3)], axis=0).astype(F32)
            for c in range(3)
        ],
        axis=1,
    )
    taps = jnp.transpose(taps).astype(BF16)
    for x in range(size_x):
        rows = []
        for y in range(0, size_y, 2):
            rhs = jnp.concatenate([stacked(cells, x, y), stacked(cells, x, y + 1)], axis=1)
            terms = jnp.dot(taps, rhs, preferred_element_type=F32)
            for k in range(2):
                part = terms[:, k * size_z : (k + 1) * size_z]
                row = shift_z(part[:channels], -1) + part[channels : 2 * channels]
                rows.append(row + shift_z(part[2 * channels :], 1))
        out_ref[:, x] = jnp.swapaxes(jnp.stack(rows), 0, 1).astype(BF16)


def shards(activation, out_grad, kernel):
    channels, size_x, size_y, size_z = activation.shape
    counts = (lax.axis_size("gx"), lax.axis_size("gy"))
    nx, ny = counts
    shape = jax.ShapeDtypeStruct
    volume = channels * size_x * size_y * size_z

    def permute(value, partner):
        return lax.ppermute(value, BOTH, pairs(counts, partner))

    def core(ix, iy):
        return ix ^ 1, iy

    def odd_x(ix, iy):
        return (ix + 1 if ix % 2 else ix - 1) % nx, iy

    def even_y(ix, iy):
        return ix, iy ^ 1

    def odd_y(ix, iy):
        if iy in (0, ny - 1):
            return ix ^ 1, iy
        return ix, (iy + 1 if iy % 2 else iy - 1)

    def call(body, out_shape, arrays, scratch=(), flops=0, in_specs=None, limit=16 << 20):
        outs = out_shape if isinstance(out_shape, tuple) else (out_shape,)
        nbytes = sum(a.size * a.dtype.itemsize for a in (*arrays, *outs))
        return pl.pallas_call(
            body,
            out_shape=out_shape,
            in_specs=in_specs or [VMEM] * len(arrays),
            out_specs=jax.tree.map(lambda _: VMEM, out_shape),
            scratch_shapes=list(scratch),
            compiler_params=params(limit),
            cost_estimate=cost(flops, nbytes),
        )(*arrays)

    face = shape((size_x, channels, size_z), BF16)
    grad, even, odd = call(gradient_body, (shape((size_x, size_y, channels, size_z), BF16), face, face), (out_grad,))
    odd = permute(odd, odd_y)
    even = permute(even, even_y)
    act = call(activation_body, shape((size_x, size_y, 3 * channels, size_z), BF16), (activation,))
    cells_shape = shape((size_x + 2, size_y + 2, channels, size_z), BF16)
    terms = shape((9 * channels, 3 * channels), F32)
    half = shape((7 * channels // 2, 4 * channels), F32)
    acc = pltpu.VMEM(terms.shape, F32)
    cells, inner = call(inner_body, (cells_shape, terms), (act, grad), flops=54 * channels * volume)
    side = shape((2 * size_y + 2, channels, size_z), BF16)
    cells, near, far, send, keep = call(
        edges_body,
        (cells_shape, side, side, half, half),
        (act, cells, inner, even, odd),
        (acc,),
        flops=12 * channels * volume,
    )
    both = nx == 4
    far = permute(far, odd_x)
    far_send, far_total = call(functools.partial(far_body, both), (half, half), (act, cells, far), (acc,), flops=volume)
    if not both:
        send, keep = send + far_send, keep + far_total
    received = permute(send, core)
    near = permute(near, core)
    total = call(near_body, half, (act, cells, near, keep, received), (acc,), flops=volume)
    if both:
        far_total = far_total + permute(far_send, core)
    step = 2
    while step < nx:
        total = total + permute(total, lambda ix, iy: (ix ^ 1 ^ step, iy))
        step *= 2
    if both:
        total = total + far_total
    grad_input = call(
        inputs_body,
        shape(activation.shape, BF16),
        (cells, near, far, kernel),
        (pltpu.VMEM(cells.shape, BF16),),
        flops=54 * channels * volume,
    )
    steps = [1 << k for k in range(ny.bit_length() - 1)]
    orders = (steps[1::-1] + steps[2:], steps[:1] + steps[2:3] + steps[1:2] + steps[3:])
    for k in range(len(steps)):

        def across_y(ix, iy):
            half = (ix ^ iy).bit_count() % 2
            return ix ^ 1, iy ^ orders[half][k]

        total = total + permute(total, across_y)
        if k == 0:
            total, grad_input = lax.optimization_barrier((total, grad_input))
    other = permute(total, core)
    cell_count = nx * size_x * ny * size_y * size_z
    finish = functools.partial(finish_body, float(cell_count) ** 0.5)

    def finished(value, mine, *before):
        return pl.pallas_call(
            finish,
            out_shape=shape(kernel.shape, F32),
            grid=(1,),
            in_specs=[VMEM] + [pl.BlockSpec(memory_space=pl.ANY)] * len(before),
            out_specs=pl.BlockSpec(
                (3, 3, 3, channels // 2, channels),
                lambda i: (0, 0, 0, half_of() if mine else 1 - half_of(), 0),
            ),
            input_output_aliases={1: 0} if before else {},
            compiler_params=params(),
            cost_estimate=cost(0, 8 * value.size),
            name="finish",
        )(value, *before)

    grad_kernel = finished(other, False, finished(total, True))
    return (grad_input, grad_kernel)


def solution(mesh):
    return jax.shard_map(
        shards,
        mesh=mesh,
        in_specs=(P(None, "gx", "gy", None), P(None, "gx", "gy", None), P()),
        out_specs=(P(None, "gx", "gy", None), P()),
        check_vma=False,
    )
```
